32 devices in a mesh: row: 4 (over z), leaf: 8 (over y, x, core).
Axes of the slice: x: 2, y: 2, z: 4, core: 2. Of those that a mesh axis runs over, the one named last changes fastest.
Arguments:
- leaf_update: float32 [16384, 256], P(('leaf', 'row')), may hold values from -6 to 6
- rhs: float32 [3, 16384, 256], P(None, ('leaf', 'row')), may hold values from -6 to 6
- inv_top: bfloat16 [2, 16384, 8, 4, 512], P(None, 'leaf', None, 'row'), may hold values from -0.03125 to 0.03125
- inv_mid: bfloat16 [2, 16384, 4, 4, 512], P(None, 'leaf', None, 'row'), may hold values from -0.046875 to 0.046875
- inv_low: bfloat16 [2, 16384, 2, 4, 512], P(None, 'leaf', None, 'row'), may hold values from -0.0625 to 0.0625
- couple_mid: bfloat16 [2, 16384, 4, 4, 512], P(None, 'leaf', None, 'row'), may hold values from -0.046875 to 0.046875
- couple_low: bfloat16 [2, 16384, 2, 4, 512], P(None, 'leaf', None, 'row'), may hold values from -0.0625 to 0.0625
- block_map: int32 [3, 128], P(None, ('leaf', 'row')), may hold values from 0 to 127, as said below
Outputs:
- solution: float32 [3, 16384, 256], P(None, ('leaf', 'row'))
- leaf_solution: float32 [16384, 256], P(('leaf', 'row'))
The draws below stay inside these ranges and needn't reach their ends.
Inputs may be any that keep to these rules, and one draw needn't show every extreme that they name: Device d of the group of a front holds rows d * 512 to (d + 1) * 512 - 1 of the front's separator part and the same rows of its update part, with d = p * 4 + r for group position p (leaf index modulo the group size) and row index r. block_map[k] is one to one within each parent, and a block held at row index r and group position p of a child lands on a parent block held at row index r and group position p or p + (group size of the parent) / 2. At level 0 every parent block receives one block.
All inputs are finite; a program needn't handle non-finite values.
Results may differ from the reference program's by a relative error of at most 0.012.
Values may be sent and summed in bfloat16 or wider, within the bound.
A program may use at most 256 MiB of HBM per device.

```python
import jax
import jax.numpy as jnp
from jax import lax

S_TOP = 16384
RHS = 128
BLOCK = 128
SLICE_ROWS = 512
BLOCKS_DEV = 4
SEP_MID = 8192
SEP_LOW = 4096
N_ROW = 4
N_LEAF = 8


def draw_block_map(key, part):
    levels = []
    for level_index in range(3):
        fronts = 2 ** level_index
        group_size = N_LEAF // fronts
        half_group = group_size // 2
        blocks_dev = BLOCKS_DEV
        per_side = blocks_dev * (2 if level_index > 0 else 1)
        pool_size = 2 * per_side
        sep_blocks = group_size * N_ROW * blocks_dev
        scores = jax.random.randint(jax.random.fold_in(key, 17 + level_index), (fronts, half_group, N_ROW, pool_size), 0, 1 << 20)
        scores = scores * pool_size + jnp.arange(pool_size, dtype=jnp.int32)
        picked = jnp.argsort(scores, axis=-1)[..., :2 * blocks_dev]
        side_index = picked // per_side
        remainder = picked % per_side
        kind_index = remainder // blocks_dev
        slot_index = remainder % blocks_dev
        position = jnp.arange(half_group, dtype=jnp.int32)[None, :, None, None]
        row_index = jnp.arange(N_ROW, dtype=jnp.int32)[None, None, :, None]
        holder = (side_index * half_group + position) * N_ROW + row_index
        targets = kind_index * sep_blocks + holder * blocks_dev + slot_index
        targets = targets.reshape(fronts, half_group, N_ROW, 2, blocks_dev).transpose(0, 3, 1, 2, 4)
        levels.append(targets.reshape(-1))
    return jnp.stack(levels).astype(jnp.int32)


def level_of(key, extent, split, low, high):
    def one(dim, blocks):
        draws = jax.random.uniform(jax.random.fold_in(jax.random.fold_in(key, 6), dim), (blocks,), jnp.float32, low / len(split), high / len(split))
        return jnp.repeat(jnp.exp(draws), extent[dim] // blocks).reshape((-1,) + (1,) * (len(extent) - dim - 1))

    level = one(*split[0])
    for cut in split[1:]:
        level = level * one(*cut)
    return level


def scatter_about(rng, dims, width, bound, pieces=(), held_as=jnp.bfloat16):
    array = jax.random.normal(rng, dims, jnp.float32) * width
    if len(pieces) > 0:
        array = level_of(rng, dims, pieces, -0.22, 0.18) * array
    return jnp.clip(array, min=-bound, max=bound).astype(held_as)


def setup_inputs(seed: int = 0) -> dict:
    key_list = jax.random.split(jax.random.key(seed), 9)
    return {
        "leaf_update": scatter_about(key_list[0], (S_TOP, 2 * RHS), 1.0, 6.0, ((0, 32),), jnp.float32),
        "rhs": scatter_about(key_list[1], (3, S_TOP, 2 * RHS), 1.0, 6.0, ((1, 32),), jnp.float32),
        "inv_top": scatter_about(key_list[2], (2, S_TOP, N_LEAF, N_ROW, SLICE_ROWS), (2 * S_TOP) ** -0.5, 0.03125, ((1, 8), (3, 4))),
        "inv_mid": scatter_about(key_list[3], (2, S_TOP, N_LEAF // 2, N_ROW, SLICE_ROWS), (2 * SEP_MID) ** -0.5, 0.046875, ((1, 8), (3, 4))),
        "inv_low": scatter_about(key_list[4], (2, S_TOP, N_LEAF // 4, N_ROW, SLICE_ROWS), (2 * SEP_LOW) ** -0.5, 0.0625, ((1, 8), (3, 4))),
        "couple_mid": scatter_about(key_list[5], (2, S_TOP, N_LEAF // 2, N_ROW, SLICE_ROWS), (2 * SEP_MID) ** -0.5, 0.046875, ((1, 8), (3, 4))),
        "couple_low": scatter_about(key_list[6], (2, S_TOP, N_LEAF // 4, N_ROW, SLICE_ROWS), (2 * SEP_LOW) ** -0.5, 0.0625, ((1, 8), (3, 4))),
        "block_map": draw_block_map(jax.random.fold_in(key_list[8], 71), 0),
    }


def complex_apply(real_part, imag_part, vector, transpose):
    half_cols = vector.shape[1] // 2
    right_side = vector.astype(jnp.bfloat16)
    if transpose:
        dim_numbers = (((0,), (0,)), ((), ()))
    else:
        dim_numbers = (((1,), (0,)), ((), ()))
    product_real = lax.dot_general(real_part, right_side, dim_numbers, preferred_element_type=jnp.float32)
    product_imag = lax.dot_general(imag_part, right_side, dim_numbers, preferred_element_type=jnp.float32)
    return jnp.concatenate([product_real[:, :half_cols] - product_imag[:, half_cols:], product_real[:, half_cols:] + product_imag[:, :half_cols]], axis=1)


def parent_index(targets, level_index, front_blocks):
    fronts = 2 ** level_index
    per_child = targets.shape[0] // (2 * fronts)
    parent_of = (jnp.arange(targets.shape[0], dtype=jnp.int32) // per_child) // 2
    return parent_of * front_blocks + targets


def reference(leaf_update, rhs, inv_top, inv_mid, inv_low, couple_mid, couple_low, block_map):
    columns = rhs.shape[2]
    inverses = [inv_top, inv_mid, inv_low]
    couplings = [None, couple_mid, couple_low]
    children = leaf_update
    saved_y = [None, None, None]
    for level_index in [2, 1, 0]:
        fronts = 2 ** level_index
        sep_rows = S_TOP // fronts
        has_update = level_index > 0
        front_blocks = (2 if has_update else 1) * (sep_rows // BLOCK)
        child_blocks = children.reshape(-1, BLOCK, columns)
        placed = parent_index(block_map[level_index], level_index, front_blocks)
        front_vec = jnp.zeros((fronts * front_blocks, BLOCK, columns), jnp.float32).at[placed].add(child_blocks)
        front_vec = front_vec.reshape(fronts, front_blocks * BLOCK, columns)
        sep_part = front_vec[:, :sep_rows] + rhs[level_index].reshape(fronts, sep_rows, columns)
        inverse = inverses[level_index].reshape(2, fronts, sep_rows, sep_rows)
        outputs_y = []
        updates = []
        for front_idx in range(fronts):
            solved = complex_apply(inverse[0, front_idx], inverse[1, front_idx], sep_part[front_idx], False)
            outputs_y.append(solved)
            if has_update:
                coupling = couplings[level_index].reshape(2, fronts, sep_rows, sep_rows)
                updates.append(front_vec[front_idx, sep_rows:] - complex_apply(coupling[0, front_idx], coupling[1, front_idx], solved, False))
        saved_y[level_index] = outputs_y
        if has_update:
            children = jnp.concatenate(updates, axis=0)
    solutions = []
    parent_flat = None
    for level_index in [0, 1, 2]:
        fronts = 2 ** level_index
        sep_rows = S_TOP // fronts
        inverse = inverses[level_index].reshape(2, fronts, sep_rows, sep_rows)
        if level_index > 0:
            parent_blocks = parent_flat.shape[0] // (2 ** (level_index - 1))
            taken_rows = parent_flat[parent_index(block_map[level_index - 1], level_index - 1, parent_blocks)]
            x_update = taken_rows.reshape(fronts, sep_rows, columns)
            coupling = couplings[level_index].reshape(2, fronts, sep_rows, sep_rows)
        level_x = []
        front_vectors = []
        for front_idx in range(fronts):
            reduced = saved_y[level_index][front_idx]
            if level_index > 0:
                reduced = reduced - complex_apply(coupling[0, front_idx], coupling[1, front_idx], x_update[front_idx], True)
            solved = complex_apply(inverse[0, front_idx], inverse[1, front_idx], reduced, True)
            level_x.append(solved)
            if level_index > 0:
                front_vectors.append(jnp.concatenate([solved, x_update[front_idx]], axis=0))
            else:
                front_vectors.append(solved)
        solutions.append(jnp.concatenate(level_x, axis=0))
        parent_flat = jnp.concatenate(front_vectors, axis=0).reshape(-1, BLOCK, columns)
    leaf_blocks = parent_flat[parent_index(block_map[2], 2, parent_flat.shape[0] // 4)]
    return jnp.stack(solutions), leaf_blocks.reshape(S_TOP, columns)
```

```python
import jax
import jax.numpy as jnp
from jax import lax
from jax.experimental import pallas as pl
from jax.experimental.pallas import tpu as pltpu
from jax.sharding import PartitionSpec as P

F32 = jnp.float32
BF16 = jnp.bfloat16
MESH = pl.DeviceIdType.MESH
HALVES = 2
GROUP = 32


def flip(value, mask):
    out, bit = value, 1
    while bit <= mask:
        if mask & bit:
            out = out + bit - 2 * bit * ((value // bit) % 2)
        bit *= 2
    return out


def span(bits):
    masks = [0]
    for bit in bits:
        masks += [mask | 1 << bit for mask in masks]
    return masks


def pick(table, index):
    total = 0
    for place, value in enumerate(table):
        total = total + jnp.where(index == place, value, 0)
    return total


class Shared:
    def __init__(self, sizes, refs):
        self.__dict__.update(sizes)
        self.__dict__.update(refs)
        self.queue = []


    def prepare(self, stage, matrix, raw, col0, pieces):
        pos, width = matrix.shape[2], self.width
        rows = raw.shape[1]
        per_part = self.panel_rows // rows
        total = 2 * per_part

        def copy(i):
            start = pl.multiple_of((i % per_part) * rows, rows)
            return pltpu.make_async_copy(
                matrix.at[i // per_part, pl.ds(start, rows)], raw.at[i % 2], self.raw_sem.at[i % 2]
            )

        def begin():
            copy(0).start()
            copy(1).start()

        def piece(first, last):
            def body(i, carry):
                copy(i).wait()
                start = (i % per_part) * rows

                def group(b, carry):
                    tile = raw[i % 2, pl.ds(pl.multiple_of(b * GROUP, GROUP), GROUP)]
                    turned = jnp.transpose(tile, (1, 0, 2))
                    where = pl.ds(pl.multiple_of(start + b * GROUP, GROUP), GROUP)
                    for p in range(pos):
                        lo = col0 + p * width
                        self.store[i // per_part, where, lo : lo + width] = turned[p]
                    return carry

                lax.fori_loop(0, rows // GROUP, group, 0)

                @pl.when(i + 2 < total)
                def _():
                    copy(i + 2).start()

                return carry

            lax.fori_loop(first, last, body, 0)

        cuts = [total * j // pieces for j in range(pieces + 1)]
        self.queue.append((stage, begin))
        for j in range(pieces):
            self.queue.append((stage, lambda a=cuts[j], b=cuts[j + 1]: piece(a, b)))

    def fill(self):
        if self.queue:
            self.queue.pop(0)[1]()

    def need(self, stage):
        while self.queue and self.queue[0][0] <= stage:
            self.fill()


class Stream:
    def __init__(self, shared, sizes, refs):
        self.__dict__.update(sizes)
        self.__dict__.update(refs)
        self.shared = shared
        self.row = lax.axis_index("row")
        self.leaf = lax.axis_index("leaf")
        self.exchange = 0


    def rows_of(self, index):
        return pl.ds(pl.multiple_of(index * self.width, self.width), self.width)

    def part_rows(self, index, part, parts):
        size = self.width // parts
        return pl.ds(pl.multiple_of(index * self.width + part * size, size), size)

    def quarter_turn(self, value):
        half = self.cols // 2
        lane = lax.broadcasted_iota(jnp.int32, value.shape, 1)
        return pltpu.roll(value, half, 1) * jnp.where(lane < half, -1.0, 1.0)

    def turn(self, par, where):
        self.turned[where] = self.quarter_turn(self.gathered[par, where].astype(F32)).astype(BF16)


    def flows(self, bits):
        if bits < 3:
            return [list(range(bits))[::-1]]
        outer = list(range(1, bits))
        return [outer + [0], outer[::-1] + [0]]

    def gather_copy(self, par, flow, count, pos, mask, bit):
        where = self.part_rows(flip(pos, mask), flow, count)
        ref = self.gathered.at[par, where]
        slot = mask ^ 1 << bit
        return pltpu.make_async_remote_copy(
            src_ref=ref,
            dst_ref=ref,
            send_sem=self.lg_send.at[flow, slot],
            recv_sem=self.lg_recv.at[par, flow, slot],
            device_id={"leaf": flip(self.leaf, 1 << bit)},
            device_id_type=MESH,
        )

    def gather_wait(self, par, flow, count, pos, mask, bit):
        where = self.part_rows(flip(pos, mask ^ 1 << bit), flow, count)
        ref = self.gathered.at[par, where]
        slot = mask ^ 1 << bit
        pltpu.make_async_remote_copy(
            src_ref=ref,
            dst_ref=ref,
            send_sem=self.lg_send.at[flow, slot],
            recv_sem=self.lg_recv.at[par, flow, slot],
            device_id={"leaf": flip(self.leaf, 1 << bit)},
            device_id_type=MESH,
        ).wait_recv()

    def gather(self, par, bits, value_ref):
        pos = self.leaf % (1 << bits)
        self.gathered[par, self.rows_of(pos)] = value_ref[...].astype(BF16)
        orders = self.flows(bits)
        count = len(orders)
        sent = []
        for step in range(bits):
            for flow, order in enumerate(orders):
                bit = order[step]
                if step > 0:
                    yield
                    for mask in span(order[: step - 1]):
                        self.gather_wait(par, flow, count, pos, mask, order[step - 1])
                for mask in span(order[:step]):
                    copy = self.gather_copy(par, flow, count, pos, mask, bit)
                    copy.start()
                    sent.append(copy)
        yield
        for flow, order in enumerate(orders):
            for mask in span(order[: bits - 1]):
                self.gather_wait(par, flow, count, pos, mask, order[bits - 1])
        return sent

    def reduce_copy(self, par, side, dest, half):
        where = self.part_rows(0, half, HALVES)
        to = self.row + 1 if side == 0 else self.row - 1
        slot = side * self.row_size + dest
        return pltpu.make_async_remote_copy(
            src_ref=self.outbox.at[dest, where],
            dst_ref=self.inbox.at[par, slot, where],
            send_sem=self.zr_send.at[dest, half],
            recv_sem=self.zr_recv.at[par, slot, half],
            device_id={"row": (to + self.row_size) % self.row_size},
            device_id_type=MESH,
        )

    def forward(self, stage, bits, col0, value_ref):
        par = stage % 2
        count, row, n = 1 << bits, self.row, self.row_size
        sent = yield from self.gather(par, bits, value_ref)
        self.shared.need(stage)
        order = []
        for r in range(n):
            order.append(sorted((d for d in range(n) if d != r), key=lambda d: -abs(d - r)) + [r])

        def one(j, carry):
            dest = 0
            for r in range(n):
                for k in range(n):
                    dest = dest + jnp.where((row == r) & (j == k), order[r][k], 0)
            where = self.rows_of(dest)
            deep = 2 * self.width

            def piece(k):
                cols = pl.ds(pl.multiple_of(col0 + k * deep, deep), deep)
                right = self.gathered[par, pl.ds(pl.multiple_of(k * deep, deep), deep)]
                real = jnp.dot(self.store[0, where, cols], right, preferred_element_type=F32)
                imag = jnp.dot(self.store[1, where, cols], right, preferred_element_type=F32)
                return real + self.quarter_turn(imag)

            self.sums[dest] = piece(0)
            if count > 2:

                def add(k, carry):
                    self.sums[dest] += piece(k)
                    return carry

                lax.fori_loop(1, count // 2, add, 0)

            @pl.when(j < n - 1)
            def _():
                @pl.when(row == 0)
                def _():
                    self.outbox[dest] = self.sums[dest].astype(BF16)
                    for half in range(HALVES):
                        self.reduce_copy(par, 0, dest, half).start()

                @pl.when(row == n - 1)
                def _():
                    self.outbox[dest] = self.sums[dest].astype(BF16)
                    for half in range(HALVES):
                        self.reduce_copy(par, 1, dest, half).start()

            return carry

        middle = n // 2 if bits > self.leaf_bits - 2 else n
        lax.fori_loop(0, middle, one, 0)
        if middle < n:
            yield
            lax.fori_loop(middle, n, one, 0)
        for copy in sent:
            copy.wait_send()

    def reduce(self, stage, out_ref, combine=None):
        par = stage % 2
        row, n = self.row, self.row_size
        for step in range(1, n):
            yield
            final = step == n - 1
            left_dest = row if final else n - 1 + row - step
            right_dest = row if final else step + 1 - n + row
            left_on = (row >= 1) & (row <= step)
            right_on = (row <= n - 2) & (row >= n - 1 - step)
            for half in range(HALVES):
                where = self.part_rows(0, half, HALVES)
                for side, dest, on in ((0, left_dest, left_on), (1, right_dest, right_on)):

                    @pl.when(on)
                    def _(side=side, dest=dest, where=where, half=half):
                        copy = self.reduce_copy(par, side, dest, half)
                        copy.wait_recv()
                        got = self.inbox[par, side * n + dest, where].astype(F32)
                        total = self.sums[dest, where] + got
                        if final:
                            self.sums[dest, where] = total
                        else:
                            self.outbox[dest, where] = total.astype(BF16)
                            copy.start()

        if combine is None:
            out_ref[...] = self.sums[row]
        else:
            out_ref[...] = combine(self.sums[row])
        for dest in range(n):
            for half in range(HALVES):

                @pl.when(row < dest)
                def _(dest=dest, half=half):
                    self.reduce_copy(par, 0, dest, half).wait_send()

                @pl.when(row > dest)
                def _(dest=dest, half=half):
                    self.reduce_copy(par, 1, dest, half).wait_send()


    def relay_copy(self, par, side, source, half):
        ref = self.gathered.at[par, self.part_rows(source, half, HALVES)]
        to = self.row + 1 if side == 0 else self.row - 1
        return pltpu.make_async_remote_copy(
            src_ref=ref,
            dst_ref=ref,
            send_sem=self.za_send.at[side, source, half],
            recv_sem=self.za_recv.at[par, source, half],
            device_id={"row": (to + self.row_size) % self.row_size},
            device_id_type=MESH,
        )

    def scatter_copy(self, par, flow, count, slot, bit):
        where = self.part_rows(0, flow, count)
        return pltpu.make_async_remote_copy(
            src_ref=self.outbox.at[slot, where],
            dst_ref=self.inbox.at[par, slot, where],
            send_sem=self.lr_send.at[flow, slot],
            recv_sem=self.lr_recv.at[par, flow, slot],
            device_id={"leaf": flip(self.leaf, 1 << bit)},
            device_id_type=MESH,
        )

    def backward(self, stage, bits, col0, value_ref):
        par = stage % 2
        count, row, n = 1 << bits, self.row, self.row_size
        self.gathered[par, self.rows_of(row)] = value_ref[...].astype(BF16)
        for half in range(HALVES):

            @pl.when(row < n - 1)
            def _(half=half):
                self.relay_copy(par, 0, row, half).start()

            @pl.when(row > 0)
            def _(half=half):
                self.relay_copy(par, 1, row, half).start()

        order = []
        for r in range(n):
            order.append(sorted(range(n), key=lambda d: abs(d - r)))

        def multiply(place):
            source = pick([order[r][place] for r in range(n)], row)
            where = self.rows_of(source)
            self.turn(par, where)

            def piece(p, carry):
                lo = pl.multiple_of(col0 + p * self.width, self.width)
                dims = (((0,), (0,)), ((), ()))
                total = lax.dot_general(
                    self.store[0, where, pl.ds(lo, self.width)],
                    self.gathered[par, where],
                    dims,
                    preferred_element_type=F32,
                ) + lax.dot_general(
                    self.store[1, where, pl.ds(lo, self.width)],
                    self.turned[where],
                    dims,
                    preferred_element_type=F32,
                )
                if place == 0:
                    self.sums[p] = total
                else:
                    self.sums[p] += total
                return carry

            lax.fori_loop(0, count, piece, 0)

        yield
        self.shared.need(stage)
        multiply(0)
        for step in range(1, n):
            yield
            for half in range(HALVES):

                @pl.when(row >= step)
                def _(half=half):
                    self.relay_copy(par, 0, row - step, half).wait_recv()

                    @pl.when(row < n - 1)
                    def _():
                        self.relay_copy(par, 0, row - step, half).start()

                @pl.when(row + step < n)
                def _(half=half):
                    self.relay_copy(par, 1, row + step, half).wait_recv()

                    @pl.when(row > 0)
                    def _():
                        self.relay_copy(par, 1, row + step, half).start()

            multiply(step)

    def scatter(self, stage, bits, out_ref, combine=None):
        par = stage % 2
        row, n = self.row, self.row_size
        pos = self.leaf % (1 << bits)
        if bits < 3:
            orders = [list(range(bits))]
        else:
            outer = list(range(1, bits))
            orders = [[0] + outer, [0] + outer[::-1]]
        flows = len(orders)
        sent = []
        base = 0
        for step in range(bits):
            pending = []
            for flow, order_bits in enumerate(orders):
                bit = order_bits[step]
                rest = order_bits[step + 1 :]
                for place, mask in enumerate(span(rest)):
                    slot = base + place
                    where = self.part_rows(0, flow, flows)
                    give = flip(pos, mask | 1 << bit)
                    self.outbox[slot, where] = self.sums[give, where].astype(BF16)
                    copy = self.scatter_copy(par, flow, flows, slot, bit)
                    copy.start()
                    sent.append(copy)
                    pending.append((copy, slot, where, flip(pos, mask)))
            yield
            for copy, slot, where, keep in pending:
                copy.wait_recv()
                self.sums[keep, where] += self.inbox[par, slot, where].astype(F32)
            base += 1 << (bits - 1 - step)
        if combine is None:
            out_ref[...] = self.sums[pos]
        else:
            out_ref[...] = combine(self.sums[pos])
        for copy in sent:
            copy.wait_send()
        for step in range(n):
            for half in range(HALVES):

                @pl.when((row >= step) & (row < n - 1))
                def _(half=half):
                    self.relay_copy(par, 0, row - step, half).wait_send()

                @pl.when((row + step < n) & (row > 0))
                def _(half=half):
                    self.relay_copy(par, 1, row + step, half).wait_send()


    def swap(self, bit):
        copy = pltpu.make_async_remote_copy(
            src_ref=self.swap_out,
            dst_ref=self.swap_in.at[self.exchange],
            send_sem=self.ex_send.at[self.exchange],
            recv_sem=self.ex_recv.at[self.exchange],
            device_id={"leaf": flip(self.leaf, 1 << bit)},
            device_id_type=MESH,
        )
        self.exchange += 1
        return copy

    def own_slots(self, bits, has_update):
        pos = self.leaf % (1 << bits)
        first = (pos * self.row_size + self.row) * self.blocks
        far = (1 << bits) * self.row_size * self.blocks
        slots = [first + s for s in range(self.blocks)]
        return slots + [slot + far for slot in slots] if has_update else slots

    def block_rows(self, j):
        return slice(j * self.block, (j + 1) * self.block)

    def extend_add(self, level, bits, child_ref, rhs_ref, sep_ref, update_ref):
        nb = self.blocks
        self.swap_out[...] = child_ref[...].astype(BF16)
        index = self.exchange
        copy = self.swap(bits - 1)
        copy.start()
        for j in range(nb):
            self.pool[j] = child_ref[self.block_rows(j), :]
        targets = [self.targets[level, j] for j in range(2 * nb)]
        yield
        copy.wait_recv()
        for j in range(nb):
            self.pool[nb + j] = self.swap_in[index, self.block_rows(j), :].astype(F32)
        for s, slot in enumerate(self.own_slots(bits, update_ref is not None)):
            place, found = 0, 0
            for j, target in enumerate(targets):
                place = jnp.where(target == slot, j, place)
                found = jnp.where(target == slot, 1, found)
            value = self.pool[place] * found.astype(F32)
            if s < nb:
                sep_ref[self.block_rows(s), :] = value + rhs_ref[level, self.block_rows(s), :]
            else:
                update_ref[self.block_rows(s - nb), :] = value
        copy.wait_send()

    def extend_down(self, level, bits, parts, out_ref):
        nb = self.blocks
        for k, part in enumerate(parts):
            for j in range(nb):
                self.pool[k * nb + j] = part[self.block_rows(j), :]
        slots = self.own_slots(bits, len(parts) > 1)

        def taken(target):
            place, found = 0, 0
            for s, slot in enumerate(slots):
                place = jnp.where(target == slot, s, place)
                found = jnp.where(target == slot, 1, found)
            return self.pool[place] * found.astype(F32)

        for j in range(nb):
            self.swap_out[self.block_rows(j), :] = taken(self.targets[level, nb + j]).astype(BF16)
        index = self.exchange
        copy = self.swap(bits - 1)
        copy.start()
        for j in range(nb):
            out_ref[self.block_rows(j), :] = taken(self.targets[level, j])
        yield
        copy.wait_recv()
        out_ref[...] += self.swap_in[index].astype(F32)
        copy.wait_send()


    def meet(self):
        barrier = pltpu.get_barrier_semaphore()
        n = self.row_size
        for bit in range(self.leaf_bits):
            pl.semaphore_signal(
                barrier, inc=1, device_id={"leaf": flip(self.leaf, 1 << bit)}, device_id_type=MESH
            )

        @pl.when(self.row > 0)
        def _():
            pl.semaphore_signal(
                barrier, inc=1, device_id={"row": self.row - 1}, device_id_type=MESH
            )

        @pl.when(self.row < n - 1)
        def _():
            pl.semaphore_signal(
                barrier, inc=1, device_id={"row": self.row + 1}, device_id_type=MESH
            )

        edge = (self.row == 0) | (self.row == n - 1)

        @pl.when(edge)
        def _():
            pl.semaphore_wait(barrier, self.leaf_bits + 1)

        @pl.when(jnp.logical_not(edge))
        def _():
            pl.semaphore_wait(barrier, self.leaf_bits + 2)

    def phases(self):
        top = self.leaf_bits
        low, mid = top - 2, top - 1
        half = (1 << top) * self.width // 2
        update, sep, solution = self.update, self.sep, self.solution

        def left(stage, bits, col0, value_ref, level=None, child=None):
            if level is not None:
                below = None if level == 0 else update
                yield from self.extend_add(level, bits, child, self.rhs, sep, below)
            yield from self.forward(stage, bits, col0, value_ref)

        def right(stage, bits, out_ref, level=None, parts=(), down_ref=None, combine=None):
            yield from self.scatter(stage, bits, out_ref, combine)
            if level is not None:
                yield from self.extend_down(level, bits, parts, down_ref)

        yield left(0, low, 0, sep, 2, self.leaf_update)
        yield self.reduce(0, self.y_low)
        yield left(1, low, half, self.y_low)
        yield self.reduce(1, update, lambda v: update[...] - v)
        yield left(2, mid, 0, sep, 1, update)
        yield self.reduce(2, self.y_mid)
        yield left(3, mid, half, self.y_mid)
        yield self.reduce(3, update, lambda v: update[...] - v)
        yield left(4, top, 0, sep, 0, update)
        yield self.reduce(4, sep)
        yield iter(())
        yield self.backward(5, top, 0, sep)
        yield right(5, top, solution.at[0], 0, [solution.at[0]], update)
        yield self.backward(6, mid, 0, update)
        yield right(6, mid, sep, combine=lambda v: self.y_mid[...] - v)
        yield self.backward(7, mid, half, sep)
        yield right(7, mid, solution.at[1], 1, [solution.at[1], update], sep)
        yield self.backward(8, low, 0, sep)
        yield right(8, low, update, combine=lambda v: self.y_low[...] - v)
        yield self.backward(9, low, half, update)
        yield right(9, low, solution.at[2], 2, [solution.at[2], sep], self.leaf_solution)


SHARED = ("inv_top", "inv_mid", "inv_low", "couple_mid", "couple_low")
SHARED += ("store", "raw_top", "raw_mid", "raw_low", "raw_sem", "targets")
NAMES = ("targets", "leaf_update", "rhs", "inv_top", "inv_mid", "inv_low")
NAMES += ("couple_mid", "couple_low", "solution", "leaf_solution")
NAMES += ("store", "raw_top", "raw_mid", "raw_low", "gathered", "turned", "inbox", "outbox")
NAMES += ("sums", "swap_in", "swap_out", "pool", "sep", "update", "y_low", "y_mid", "raw_sem")
NAMES += ("lg_send", "lg_recv", "zr_send", "zr_recv", "za_send", "za_recv")
NAMES += ("lr_send", "lr_recv", "ex_send", "ex_recv")
STREAMS = 2


def kernel(sizes, *refs):
    refs = dict(zip(NAMES, refs, strict=True))
    common = {name: refs[name] for name in SHARED}
    shared = Shared(sizes, common)
    streams = []
    for f in range(STREAMS):
        own = {name: ref.at[f] for name, ref in refs.items() if name not in SHARED}
        streams.append(Stream(shared, sizes, own | common))
    half = (1 << sizes["leaf_bits"]) * sizes["width"] // 2
    due = {
        0: [(0, shared.inv_low, shared.raw_low, 0, 1), (1, shared.couple_low, shared.raw_low, half, 2)],
        2: [(2, shared.inv_mid, shared.raw_mid, 0, 4)],
        4: [(3, shared.couple_mid, shared.raw_mid, half, 4)],
        8: [(4, shared.inv_top, shared.raw_top, 0, 6)],
        13: [
            (6, shared.couple_mid, shared.raw_mid, 0, 2),
            (7, shared.inv_mid, shared.raw_mid, half, 4),
        ],
        15: [(8, shared.couple_low, shared.raw_low, 0, 3)],
        17: [(9, shared.inv_low, shared.raw_low, half, 3)],
    }
    for item in due.pop(0):
        shared.prepare(*item)
    shared.fill()
    streams[0].meet()
    lists = [list(stream.phases()) for stream in streams]
    for macro in range(len(lists[0]) + 1):
        for item in due.get(macro, ()):
            shared.prepare(*item)
        live = []
        if macro < len(lists[0]):
            live.append(lists[0][macro])
        if macro > 0:
            live.append(lists[1][macro - 1])
        while live:
            for phase in list(live):
                if next(phase, True):
                    live.remove(phase)
                shared.fill()


def shards(leaf_update, rhs, inv_top, inv_mid, inv_low, couple_mid, couple_low, block_map):
    row_size, leaf_size = lax.axis_size("row"), lax.axis_size("leaf")
    leaf_bits = leaf_size.bit_length() - 1
    width, cols = leaf_update.shape
    blocks = block_map.shape[1]
    panel_rows = inv_top.shape[1]
    partner = []
    for level in range(3):
        bit = leaf_bits - level - 1
        route = [(i, i ^ 1 << bit) for i in range(leaf_size)]
        partner.append(lax.ppermute(block_map[level], "leaf", route))
    targets = jnp.concatenate([block_map, jnp.stack(partner)], axis=1)

    quarter = cols // 4

    def split(array):
        parts = array.reshape(*array.shape[:-1], 2, STREAMS, quarter)
        return jnp.moveaxis(parts, -2, 0).reshape(STREAMS, *array.shape[:-1], 2 * quarter)

    def joined(array):
        parts = array.reshape(*array.shape[:-1], 2, quarter)
        return jnp.moveaxis(parts, 0, -2).reshape(*array.shape[1:-1], 4 * quarter)

    def flat(matrix):
        return matrix.reshape(2, panel_rows, matrix.shape[2], width)

    matrices = [flat(m) for m in (inv_top, inv_mid, inv_low, couple_mid, couple_low)]
    sizes = dict(
        row_size=row_size,
        leaf_bits=leaf_bits,
        width=width,
        cols=cols // STREAMS,
        blocks=blocks,
        block=width // blocks,
        panel_rows=panel_rows,
    )
    slots = max(leaf_size, 2 * row_size)
    chunk = min(256, panel_rows // 2)
    vmem = pl.BlockSpec(memory_space=pltpu.VMEM)
    hbm = pl.BlockSpec(memory_space=pl.ANY)
    dma = pltpu.SemaphoreType.DMA
    cols = cols // STREAMS
    most = max(leaf_size, row_size)

    def each(*shape, dtype=F32):
        return pltpu.VMEM((STREAMS, *shape), dtype)

    solutions, leaf_solution = pl.pallas_call(
        lambda *refs: kernel(sizes, *refs),
        out_shape=(
            jax.ShapeDtypeStruct((STREAMS, 3, width, cols), F32),
            jax.ShapeDtypeStruct((STREAMS, width, cols), F32),
        ),
        in_specs=[pl.BlockSpec(memory_space=pltpu.SMEM), vmem, vmem] + [hbm] * 5,
        out_specs=(vmem, vmem),
        scratch_shapes=[
            pltpu.VMEM((2, panel_rows, leaf_size * width), BF16),
            pltpu.VMEM((2, chunk // 2, leaf_size, width), BF16),
            pltpu.VMEM((2, chunk, leaf_size // 2, width), BF16),
            pltpu.VMEM((2, chunk, leaf_size // 4, width), BF16),
            each(2, most * width, cols, dtype=BF16),
            each(row_size * width, cols, dtype=BF16),
            each(2, slots, width, cols, dtype=BF16),
            each(most, width, cols, dtype=BF16),
            each(most, width, cols),
            each(6, width, cols, dtype=BF16),
            each(width, cols, dtype=BF16),
            each(2 * blocks, width // blocks, cols),
            each(width, cols),
            each(width, cols),
            each(width, cols),
            each(width, cols),
            dma((2,)),
            dma((STREAMS, 2, leaf_size)),
            dma((STREAMS, 2, 2, leaf_size)),
            dma((STREAMS, row_size, HALVES)),
            dma((STREAMS, 2, 2 * row_size, HALVES)),
            dma((STREAMS, 2, row_size, HALVES)),
            dma((STREAMS, 2, row_size, HALVES)),
            dma((STREAMS, 2, leaf_size)),
            dma((STREAMS, 2, 2, leaf_size)),
            dma((STREAMS, 6)),
            dma((STREAMS, 6)),
        ],
        compiler_params=pltpu.CompilerParams(
            collective_id=0, has_side_effects=True, vmem_limit_bytes=67043328
        ),
    )(targets, split(leaf_update), split(rhs), *matrices)
    return joined(solutions), joined(leaf_solution)


def solution(mesh):
    return jax.shard_map(
        shards,
        mesh=mesh,
        in_specs=(
            P(("leaf", "row"), None),
            P(None, ("leaf", "row"), None),
            P(None, "leaf", None, "row", None),
            P(None, "leaf", None, "row", None),
            P(None, "leaf", None, "row", None),
            P(None, "leaf", None, "row", None),
            P(None, "leaf", None, "row", None),
            P(None, ("leaf", "row")),
        ),
        out_specs=(P(None, ("leaf", "row"), None), P(("leaf", "row"), None)),
        check_vma=False,
    )
```

```python
import jax
import jax.numpy as jnp
from jax import lax
from jax.experimental import pallas as pl
from jax.experimental.pallas import tpu as pltpu
from jax.sharding import PartitionSpec as P

F32 = jnp.float32
BF16 = jnp.bfloat16
MESH = pl.DeviceIdType.MESH
HALVES = 2
GROUP = 32


def flip(value, mask):
    out, bit = value, 1
    while bit <= mask:
        if mask & bit:
            out = out + bit - 2 * bit * ((value // bit) % 2)
        bit *= 2
    return out


def span(bits):
    masks = [0]
    for bit in bits:
        masks += [mask | 1 << bit for mask in masks]
    return masks


def pick(table, index):
    total = 0
    for place, value in enumerate(table):
        total = total + jnp.where(index == place, value, 0)
    return total


class Step:
    def __init__(self, sizes, refs):
        self.__dict__.update(sizes)
        self.__dict__.update(refs)
        self.row = lax.axis_index("row")
        self.leaf = lax.axis_index("leaf")
        self.queue = []
        self.stage = 0
        self.exchange = 0


    def prepare(self, matrix, raw, col0, pieces, late=False):
        pos, width = matrix.shape[2], self.width
        rows = raw.shape[1]
        per_part = self.panel_rows // rows
        total = 2 * per_part

        def copy(i):
            start = pl.multiple_of((i % per_part) * rows, rows)
            return pltpu.make_async_copy(
                matrix.at[i // per_part, pl.ds(start, rows)], raw.at[i % 2], self.raw_sem.at[i % 2]
            )

        def begin():
            copy(0).start()
            copy(1).start()

        def piece(first, last):
            def body(i, carry):
                copy(i).wait()
                start = (i % per_part) * rows

                def group(b, carry):
                    tile = raw[i % 2, pl.ds(pl.multiple_of(b * GROUP, GROUP), GROUP)]
                    turned = jnp.transpose(tile, (1, 0, 2))
                    where = pl.ds(pl.multiple_of(start + b * GROUP, GROUP), GROUP)
                    for p in range(pos):
                        lo = col0 + p * width
                        self.store[i // per_part, where, lo : lo + width] = turned[p]
                    return carry

                lax.fori_loop(0, rows // GROUP, group, 0)

                @pl.when(i + 2 < total)
                def _():
                    copy(i + 2).start()

                return carry

            lax.fori_loop(first, last, body, 0)

        cuts = [total * j // pieces for j in range(pieces + 1)]
        if not late:
            begin()
        else:
            self.queue.append(begin)
        for j in range(pieces):
            self.queue.append(lambda a=cuts[j], b=cuts[j + 1]: piece(a, b))

    def fill(self):
        if self.queue:
            self.queue.pop(0)()

    def flush(self):
        while self.queue:
            self.fill()


    def rows_of(self, index):
        return pl.ds(pl.multiple_of(index * self.width, self.width), self.width)

    def part_rows(self, index, part, parts):
        size = self.width // parts
        return pl.ds(pl.multiple_of(index * self.width + part * size, size), size)

    def turn(self, par, where):
        half = self.cols // 2
        block = self.gathered[par, where]
        self.turned[where, :half] = -block[:, half:]
        self.turned[where, half:] = block[:, :half]


    def flows(self, bits):
        if bits < 3:
            return [list(range(bits))[::-1]]
        outer = list(range(1, bits))
        return [outer + [0], outer[::-1] + [0]]

    def gather_copy(self, par, flow, count, pos, mask, bit):
        where = self.part_rows(flip(pos, mask), flow, count)
        ref = self.gathered.at[par, where]
        slot = mask ^ 1 << bit
        return pltpu.make_async_remote_copy(
            src_ref=ref,
            dst_ref=ref,
            send_sem=self.lg_send.at[flow, slot],
            recv_sem=self.lg_recv.at[par, flow, slot],
            device_id={"leaf": flip(self.leaf, 1 << bit)},
            device_id_type=MESH,
        )

    def gather_wait(self, par, flow, count, pos, mask, bit):
        where = self.part_rows(flip(pos, mask ^ 1 << bit), flow, count)
        ref = self.gathered.at[par, where]
        slot = mask ^ 1 << bit
        pltpu.make_async_remote_copy(
            src_ref=ref,
            dst_ref=ref,
            send_sem=self.lg_send.at[flow, slot],
            recv_sem=self.lg_recv.at[par, flow, slot],
            device_id={"leaf": flip(self.leaf, 1 << bit)},
            device_id_type=MESH,
        ).wait_recv()

    def gather(self, par, bits, value_ref):
        pos = self.leaf % (1 << bits)
        self.gathered[par, self.rows_of(pos)] = value_ref[...].astype(BF16)
        orders = self.flows(bits)
        count = len(orders)
        sent = []

        def send(flow, mask, bit):
            copy = self.gather_copy(par, flow, count, pos, mask, bit)
            copy.start()
            sent.append(copy)

        for step in range(bits):
            for flow, order in enumerate(orders):
                send(flow, 0, order[step])
        self.turn(par, self.rows_of(pos))
        for step in range(bits):
            for flow, order in enumerate(orders):
                for mask in span(order[:step]):
                    self.gather_wait(par, flow, count, pos, mask, order[step])
                    for bit in order[step + 1 :]:
                        send(flow, mask | 1 << order[step], bit)
        return sent

    def reduce_copy(self, par, side, dest, half):
        where = self.part_rows(0, half, HALVES)
        to = self.row + 1 if side == 0 else self.row - 1
        slot = side * self.row_size + dest
        return pltpu.make_async_remote_copy(
            src_ref=self.outbox.at[dest, where],
            dst_ref=self.inbox.at[par, slot, where],
            send_sem=self.zr_send.at[dest, half],
            recv_sem=self.zr_recv.at[par, slot, half],
            device_id={"row": (to + self.row_size) % self.row_size},
            device_id_type=MESH,
        )

    def forward(self, bits, col0, value_ref, out_ref, following=None, combine=None):
        par = self.stage % 2
        self.stage += 1
        count, row, n = 1 << bits, self.row, self.row_size
        depth = count * self.width
        sent = self.gather(par, bits, value_ref)
        pos = self.leaf % count

        def turn_piece(j, carry):
            self.turn(par, self.rows_of((pos + j) % count))
            return carry

        lax.fori_loop(1, count, turn_piece, 0)
        self.flush()
        if following:
            self.prepare(*following)
        order = []
        for r in range(n):
            order.append(sorted((d for d in range(n) if d != r), key=lambda d: -abs(d - r)) + [r])

        def one(j, carry):
            dest = 0
            for r in range(n):
                for k in range(n):
                    dest = dest + jnp.where((row == r) & (j == k), order[r][k], 0)
            where = self.rows_of(dest)
            total = jnp.dot(
                self.store[0, where, col0 : col0 + depth],
                self.gathered[par, :depth],
                preferred_element_type=F32,
            ) + jnp.dot(
                self.store[1, where, col0 : col0 + depth],
                self.turned[:depth],
                preferred_element_type=F32,
            )
            self.sums[dest] = total

            @pl.when(j < n - 1)
            def _():
                @pl.when(row == 0)
                def _():
                    self.outbox[dest] = total.astype(BF16)
                    for half in range(HALVES):
                        self.reduce_copy(par, 0, dest, half).start()

                @pl.when(row == n - 1)
                def _():
                    self.outbox[dest] = total.astype(BF16)
                    for half in range(HALVES):
                        self.reduce_copy(par, 1, dest, half).start()

            return carry

        lax.fori_loop(0, n, one, 0)
        for copy in sent:
            copy.wait_send()
        for step in range(1, n):
            self.fill()
            final = step == n - 1
            left_dest = row if final else n - 1 + row - step
            right_dest = row if final else step + 1 - n + row
            left_on = (row >= 1) & (row <= step)
            right_on = (row <= n - 2) & (row >= n - 1 - step)
            for half in range(HALVES):
                where = self.part_rows(0, half, HALVES)
                for side, dest, on in ((0, left_dest, left_on), (1, right_dest, right_on)):

                    @pl.when(on)
                    def _(side=side, dest=dest, where=where, half=half):
                        copy = self.reduce_copy(par, side, dest, half)
                        copy.wait_recv()
                        got = self.inbox[par, side * n + dest, where].astype(F32)
                        total = self.sums[dest, where] + got
                        if final:
                            self.sums[dest, where] = total
                        else:
                            self.outbox[dest, where] = total.astype(BF16)
                            copy.start()

        if combine is None:
            out_ref[...] = self.sums[row]
        else:
            out_ref[...] = combine(self.sums[row])
        for dest in range(n):
            for half in range(HALVES):

                @pl.when(row < dest)
                def _(dest=dest, half=half):
                    self.reduce_copy(par, 0, dest, half).wait_send()

                @pl.when(row > dest)
                def _(dest=dest, half=half):
                    self.reduce_copy(par, 1, dest, half).wait_send()


    def relay_copy(self, par, side, source, half):
        ref = self.gathered.at[par, self.part_rows(source, half, HALVES)]
        to = self.row + 1 if side == 0 else self.row - 1
        return pltpu.make_async_remote_copy(
            src_ref=ref,
            dst_ref=ref,
            send_sem=self.za_send.at[side, source, half],
            recv_sem=self.za_recv.at[par, source, half],
            device_id={"row": (to + self.row_size) % self.row_size},
            device_id_type=MESH,
        )

    def scatter_copy(self, par, flow, count, slot, bit):
        where = self.part_rows(0, flow, count)
        return pltpu.make_async_remote_copy(
            src_ref=self.outbox.at[slot, where],
            dst_ref=self.inbox.at[par, slot, where],
            send_sem=self.lr_send.at[flow, slot],
            recv_sem=self.lr_recv.at[par, flow, slot],
            device_id={"leaf": flip(self.leaf, 1 << bit)},
            device_id_type=MESH,
        )

    def backward(self, bits, col0, value, out_ref, combine=None):
        par = self.stage % 2
        self.stage += 1
        count, row, n = 1 << bits, self.row, self.row_size
        pos = self.leaf % count
        self.gathered[par, self.rows_of(row)] = value.astype(BF16)
        for half in range(HALVES):

            @pl.when(row < n - 1)
            def _(half=half):
                self.relay_copy(par, 0, row, half).start()

            @pl.when(row > 0)
            def _(half=half):
                self.relay_copy(par, 1, row, half).start()

        order = []
        for r in range(n):
            order.append(sorted(range(n), key=lambda d: abs(d - r)))

        def multiply(place):
            source = pick([order[r][place] for r in range(n)], row)
            where = self.rows_of(source)
            self.turn(par, where)

            def piece(p, carry):
                lo = pl.multiple_of(col0 + p * self.width, self.width)
                dims = (((0,), (0,)), ((), ()))
                total = lax.dot_general(
                    self.store[0, where, pl.ds(lo, self.width)],
                    self.gathered[par, where],
                    dims,
                    preferred_element_type=F32,
                ) + lax.dot_general(
                    self.store[1, where, pl.ds(lo, self.width)],
                    self.turned[where],
                    dims,
                    preferred_element_type=F32,
                )
                if place == 0:
                    self.sums[p] = total
                else:
                    self.sums[p] += total
                return carry

            lax.fori_loop(0, count, piece, 0)

        self.flush_own()
        multiply(0)
        for step in range(1, n):
            self.fill()
            for half in range(HALVES):

                @pl.when(row >= step)
                def _(half=half):
                    self.relay_copy(par, 0, row - step, half).wait_recv()

                    @pl.when(row < n - 1)
                    def _():
                        self.relay_copy(par, 0, row - step, half).start()

                @pl.when(row + step < n)
                def _(half=half):
                    self.relay_copy(par, 1, row + step, half).wait_recv()

                    @pl.when(row > 0)
                    def _():
                        self.relay_copy(par, 1, row + step, half).start()

            multiply(step)
        if bits < 3:
            orders = [list(range(bits))]
        else:
            outer = list(range(1, bits))
            orders = [[0] + outer, [0] + outer[::-1]]
        flows = len(orders)
        sent = []
        base = 0
        for step in range(bits):
            pending = []
            for flow, order_bits in enumerate(orders):
                bit = order_bits[step]
                rest = order_bits[step + 1 :]
                for place, mask in enumerate(span(rest)):
                    slot = base + place
                    where = self.part_rows(0, flow, flows)
                    give = flip(pos, mask | 1 << bit)
                    self.outbox[slot, where] = self.sums[give, where].astype(BF16)
                    copy = self.scatter_copy(par, flow, flows, slot, bit)
                    copy.start()
                    sent.append(copy)
                    pending.append((copy, slot, where, flip(pos, mask)))
            self.fill()
            for copy, slot, where, keep in pending:
                copy.wait_recv()
                self.sums[keep, where] += self.inbox[par, slot, where].astype(F32)
            base += 1 << (bits - 1 - step)
        if combine is None:
            out_ref[...] = self.sums[pos]
        else:
            out_ref[...] = combine(self.sums[pos])
        for copy in sent:
            copy.wait_send()
        for step in range(n):
            for half in range(HALVES):

                @pl.when((row >= step) & (row < n - 1))
                def _(half=half):
                    self.relay_copy(par, 0, row - step, half).wait_send()

                @pl.when((row + step < n) & (row > 0))
                def _(half=half):
                    self.relay_copy(par, 1, row + step, half).wait_send()

    def flush_own(self):
        while self.queue and self.must > 0:
            self.must -= 1
            self.fill()


    def swap(self, bit):
        copy = pltpu.make_async_remote_copy(
            src_ref=self.swap_out,
            dst_ref=self.swap_in.at[self.exchange],
            send_sem=self.ex_send.at[self.exchange],
            recv_sem=self.ex_recv.at[self.exchange],
            device_id={"leaf": flip(self.leaf, 1 << bit)},
            device_id_type=MESH,
        )
        self.exchange += 1
        return copy

    def own_slots(self, bits, has_update):
        pos = self.leaf % (1 << bits)
        first = (pos * self.row_size + self.row) * self.blocks
        far = (1 << bits) * self.row_size * self.blocks
        slots = [first + s for s in range(self.blocks)]
        return slots + [slot + far for slot in slots] if has_update else slots

    def block_rows(self, j):
        return slice(j * self.block, (j + 1) * self.block)

    def extend_add(self, level, bits, child_ref, rhs_ref, sep_ref, update_ref):
        nb = self.blocks
        self.swap_out[...] = child_ref[...].astype(BF16)
        index = self.exchange
        copy = self.swap(bits - 1)
        copy.start()
        for j in range(nb):
            self.pool[j] = child_ref[self.block_rows(j), :]
        targets = [self.targets[level, j] for j in range(2 * nb)]
        self.fill()
        copy.wait_recv()
        for j in range(nb):
            self.pool[nb + j] = self.swap_in[index, self.block_rows(j), :].astype(F32)
        for s, slot in enumerate(self.own_slots(bits, update_ref is not None)):
            place, found = 0, 0
            for j, target in enumerate(targets):
                place = jnp.where(target == slot, j, place)
                found = jnp.where(target == slot, 1, found)
            value = self.pool[place] * found.astype(F32)
            if s < nb:
                sep_ref[self.block_rows(s), :] = value + rhs_ref[level, self.block_rows(s), :]
            else:
                update_ref[self.block_rows(s - nb), :] = value
        copy.wait_send()

    def extend_down(self, level, bits, parts, out_ref):
        nb = self.blocks
        for k, part in enumerate(parts):
            for j in range(nb):
                self.pool[k * nb + j] = part[self.block_rows(j), :]
        slots = self.own_slots(bits, len(parts) > 1)

        def taken(target):
            place, found = 0, 0
            for s, slot in enumerate(slots):
                place = jnp.where(target == slot, s, place)
                found = jnp.where(target == slot, 1, found)
            return self.pool[place] * found.astype(F32)

        for j in range(nb):
            self.swap_out[self.block_rows(j), :] = taken(self.targets[level, nb + j]).astype(BF16)
        index = self.exchange
        copy = self.swap(bits - 1)
        copy.start()
        for j in range(nb):
            out_ref[self.block_rows(j), :] = taken(self.targets[level, j])
        self.fill()
        copy.wait_recv()
        out_ref[...] += self.swap_in[index].astype(F32)
        copy.wait_send()


    def meet(self):
        barrier = pltpu.get_barrier_semaphore()
        n = self.row_size
        for bit in range(self.leaf_bits):
            pl.semaphore_signal(
                barrier, inc=1, device_id={"leaf": flip(self.leaf, 1 << bit)}, device_id_type=MESH
            )

        @pl.when(self.row > 0)
        def _():
            pl.semaphore_signal(
                barrier, inc=1, device_id={"row": self.row - 1}, device_id_type=MESH
            )

        @pl.when(self.row < n - 1)
        def _():
            pl.semaphore_signal(
                barrier, inc=1, device_id={"row": self.row + 1}, device_id_type=MESH
            )

        edge = (self.row == 0) | (self.row == n - 1)

        @pl.when(edge)
        def _():
            pl.semaphore_wait(barrier, self.leaf_bits + 1)

        @pl.when(jnp.logical_not(edge))
        def _():
            pl.semaphore_wait(barrier, self.leaf_bits + 2)

    def run(self):
        top, bits = self.leaf_bits, self.leaf_bits
        low, mid = bits - 2, bits - 1
        half = (1 << top) * self.width // 2
        steps = self.row_size - 1
        self.must = 0
        self.prepare(self.inv_low, self.raw_low, 0, 2)
        self.meet()
        self.extend_add(2, low, self.leaf_update, self.rhs, self.sep, self.update)
        self.flush()
        following = (self.couple_low, self.raw_low, half, steps)
        self.forward(low, 0, self.sep, self.y_low, following)
        update = self.update
        following = (self.inv_mid, self.raw_mid, 0, steps)
        self.forward(low, half, self.y_low, self.update, following, lambda v: update[...] - v)
        self.extend_add(1, mid, self.update, self.rhs, self.sep, self.update)
        following = (self.couple_mid, self.raw_mid, half, steps)
        self.forward(mid, 0, self.sep, self.y_mid, following)
        following = (self.inv_top, self.raw_top, 0, steps)
        self.forward(mid, half, self.y_mid, self.update, following, lambda v: update[...] - v)
        self.extend_add(0, top, self.update, self.rhs, self.sep, None)
        self.forward(top, 0, self.sep, self.sep)
        solution = self.solution
        self.backward(top, 0, self.sep[...], solution.at[0])
        self.prepare(self.couple_mid, self.raw_mid, 0, 2)
        self.extend_down(0, top, [solution.at[0]], self.update)
        self.must = len(self.queue)
        self.prepare(self.inv_mid, self.raw_mid, half, steps, late=True)
        y_mid, y_low = self.y_mid, self.y_low
        self.backward(mid, 0, self.update[...], self.sep, lambda v: y_mid[...] - v)
        self.flush()
        self.prepare(self.couple_low, self.raw_low, 0, steps)
        self.backward(mid, half, self.sep[...], solution.at[1])
        self.flush()
        self.extend_down(1, mid, [solution.at[1], self.update], self.sep)
        self.prepare(self.inv_low, self.raw_low, half, steps)
        self.backward(low, 0, self.sep[...], self.update, lambda v: y_low[...] - v)
        self.flush()
        self.backward(low, half, self.update[...], solution.at[2])
        self.extend_down(2, low, [solution.at[2], self.sep], self.leaf_solution)


NAMES = ("targets", "leaf_update", "rhs", "inv_top", "inv_mid", "inv_low")
NAMES += ("couple_mid", "couple_low", "solution", "leaf_solution")
NAMES += ("store", "raw_top", "raw_mid", "raw_low", "gathered", "turned", "inbox", "outbox")
NAMES += ("sums", "swap_in", "swap_out", "pool", "sep", "update", "y_low", "y_mid", "raw_sem")
NAMES += ("lg_send", "lg_recv", "zr_send", "zr_recv", "za_send", "za_recv")
NAMES += ("lr_send", "lr_recv", "ex_send", "ex_recv")


def kernel(sizes, *refs):
    Step(sizes, dict(zip(NAMES, refs, strict=True))).run()


def shards(leaf_update, rhs, inv_top, inv_mid, inv_low, couple_mid, couple_low, block_map):
    row_size, leaf_size = lax.axis_size("row"), lax.axis_size("leaf")
    leaf_bits = leaf_size.bit_length() - 1
    width, cols = leaf_update.shape
    blocks = block_map.shape[1]
    panel_rows = inv_top.shape[1]
    partner = []
    for level in range(3):
        bit = leaf_bits - level - 1
        route = [(i, i ^ 1 << bit) for i in range(leaf_size)]
        partner.append(lax.ppermute(block_map[level], "leaf", route))
    targets = jnp.concatenate([block_map, jnp.stack(partner)], axis=1)

    def flat(matrix):
        return matrix.reshape(2, panel_rows, matrix.shape[2], width)

    matrices = [flat(m) for m in (inv_top, inv_mid, inv_low, couple_mid, couple_low)]
    sizes = dict(
        row_size=row_size,
        leaf_bits=leaf_bits,
        width=width,
        cols=cols,
        blocks=blocks,
        block=width // blocks,
        panel_rows=panel_rows,
    )
    slots = max(leaf_size, 2 * row_size)
    chunk = min(256, panel_rows // 2)
    vmem = pl.BlockSpec(memory_space=pltpu.VMEM)
    hbm = pl.BlockSpec(memory_space=pl.ANY)
    dma = pltpu.SemaphoreType.DMA
    tile = (width, cols)
    return pl.pallas_call(
        lambda *refs: kernel(sizes, *refs),
        out_shape=(
            jax.ShapeDtypeStruct((3, width, cols), F32),
            jax.ShapeDtypeStruct((width, cols), F32),
        ),
        in_specs=[pl.BlockSpec(memory_space=pltpu.SMEM), vmem, vmem] + [hbm] * 5,
        out_specs=(vmem, vmem),
        scratch_shapes=[
            pltpu.VMEM((2, panel_rows, leaf_size * width), BF16),
            pltpu.VMEM((2, chunk // 2, leaf_size, width), BF16),
            pltpu.VMEM((2, chunk, leaf_size // 2, width), BF16),
            pltpu.VMEM((2, chunk, leaf_size // 4, width), BF16),
            pltpu.VMEM((2, max(leaf_size, row_size) * width, cols), BF16),
            pltpu.VMEM((max(leaf_size, row_size) * width, cols), BF16),
            pltpu.VMEM((2, slots, width, cols), BF16),
            pltpu.VMEM((max(leaf_size, row_size), width, cols), BF16),
            pltpu.VMEM((max(leaf_size, row_size), width, cols), F32),
            pltpu.VMEM((6, width, cols), BF16),
            pltpu.VMEM((width, cols), BF16),
            pltpu.VMEM((2 * blocks, width // blocks, cols), F32),
            pltpu.VMEM(tile, F32),
            pltpu.VMEM(tile, F32),
            pltpu.VMEM(tile, F32),
            pltpu.VMEM(tile, F32),
            dma((2,)),
            dma((2, leaf_size)),
            dma((2, 2, leaf_size)),
            dma((row_size, HALVES)),
            dma((2, 2 * row_size, HALVES)),
            dma((2, row_size, HALVES)),
            dma((2, row_size, HALVES)),
            dma((2, leaf_size)),
            dma((2, 2, leaf_size)),
            dma((6,)),
            dma((6,)),
        ],
        compiler_params=pltpu.CompilerParams(
            collective_id=0, has_side_effects=True, vmem_limit_bytes=67043328
        ),
    )(targets, leaf_update, rhs, *matrices)


def solution(mesh):
    return jax.shard_map(
        shards,
        mesh=mesh,
        in_specs=(
            P(("leaf", "row"), None),
            P(None, ("leaf", "row"), None),
            P(None, "leaf", None, "row", None),
            P(None, "leaf", None, "row", None),
            P(None, "leaf", None, "row", None),
            P(None, "leaf", None, "row", None),
            P(None, "leaf", None, "row", None),
            P(None, ("leaf", "row")),
        ),
        out_specs=(P(None, ("leaf", "row"), None), P(("leaf", "row"), None)),
        check_vma=False,
    )
```
